32 devices in a mesh: groups: 2 (over y), ctx: 4 (over z), segment: 2 (over x), head: 2 (over core).
Axes of the slice: x: 2, y: 2, z: 4, core: 2. Of those that a mesh axis runs over, the one named last changes fastest.
Arguments:
- queries: bfloat16 [4, 2048, 4096], P(('groups', 'segment'), 'ctx', 'head'), parts along dimension 0, may hold values from -16 to 16
- span_key_values: bfloat16 [4, 2048, 2, 1024], P(('groups', 'segment'), 'ctx', None, 'head'), parts along dimension 0, may hold values from -6 to 6
- key_value_cache: bfloat16 [4, 16384, 2, 1024], P(('groups', 'segment'), 'ctx', None, 'head'), parts along dimension 0, may hold values from -12 to 12
- chosen: int32 [4, 4, 8, 8], P(('groups', 'segment'), None, 'head'), parts along dimension 0, may hold values from 0 to 31, as said below
- offset: int32 [4], P(('groups', 'segment')), parts along dimension 0, may hold values from 8192 to 16384, as said below
Outputs:
- handed: bfloat16 [4, 2048, 4096], P(('groups', 'segment'), 'ctx', 'head'), parts along dimension 0
The draws below stay inside these ranges and needn't reach their ends.
There are 2 independent parts, one for each index of `groups`. The reference program is written for one: setup_inputs(seed, part) draws one part's arguments, and reference() takes and returns one part's arrays. A program takes and returns all parts, laid end to end along the dimension named above; each array names one. Nothing has to cross between parts.
Inputs may be any that keep to these rules, and one draw needn't show every extreme that they name: `offset`: the first section's span starts at 16384; every other section's at 512 times a whole number from 16 to 32. `chosen`: for a section whose span starts at o, each query block and KV head names 8 different cache blocks below o / 512, among them block 0 and block o / 512 - 1.
All inputs are finite; a program needn't handle non-finite values.
Results may differ from the reference program's by a relative error of at most 0.0085.
Values may be sent and summed in bfloat16 or wider, within the bound.
A program may use at most 128 MiB of HBM per device.

```python
import jax
import jax.numpy as jnp
from jax import lax

HEAD_SIZE = 128
QUERY_HEADS = 32
VALUE_HEADS = 8
BLOCK_TOKENS = 512
CHOSEN_BLOCKS = 8
QUERY_BLOCKS = 4
CACHE_BLOCKS = 32
SPAN_TOKENS = 2048
CACHE_SLOTS = 16384
N_SEGMENT = 2


def section_blocks(key):
    drawn = jax.random.randint(jax.random.fold_in(key, 101), (N_SEGMENT,), CACHE_BLOCKS // 2, CACHE_BLOCKS + 1)
    leading = jnp.arange(N_SEGMENT) == 0
    return jnp.where(leading, CACHE_BLOCKS, drawn).astype(jnp.int32)


def draw_offset(key, part):
    return (section_blocks(key) * BLOCK_TOKENS).astype(jnp.int32)


def draw_chosen(key, part):
    valid_mask = section_blocks(key)[:, None, None, None]
    index = jnp.arange(CACHE_BLOCKS, dtype=jnp.int32)
    random_jitter = jax.random.randint(jax.random.fold_in(key, 202), (N_SEGMENT, QUERY_BLOCKS, VALUE_HEADS, CACHE_BLOCKS), 0, 2 ** 20)
    priority = random_jitter * CACHE_BLOCKS + index
    usable = (index >= 1) & (index < valid_mask - 1)
    priority = jnp.where(usable, priority, -1 - index)
    _, picked = lax.top_k(priority, CHOSEN_BLOCKS - 2)
    zero_column = jnp.zeros((N_SEGMENT, QUERY_BLOCKS, VALUE_HEADS, 1), jnp.int32)
    newest_entry = jnp.broadcast_to(valid_mask - 1, (N_SEGMENT, QUERY_BLOCKS, VALUE_HEADS, 1)).astype(jnp.int32)
    joined = jnp.concatenate([zero_column, newest_entry, picked.astype(jnp.int32)], axis=-1)
    ordering_jitter = jax.random.randint(jax.random.fold_in(key, 303), (N_SEGMENT, QUERY_BLOCKS, VALUE_HEADS, CHOSEN_BLOCKS), 0, 2 ** 20) * CHOSEN_BLOCKS + jnp.arange(CHOSEN_BLOCKS, dtype=jnp.int32)
    order = jnp.argsort(ordering_jitter, axis=-1, stable=True)
    return jnp.take_along_axis(joined, order, axis=-1).astype(jnp.int32)


def draw_queries(key, part):
    array_shape = (N_SEGMENT, SPAN_TOKENS, QUERY_HEADS * HEAD_SIZE)
    drawn = jax.random.normal(jax.random.fold_in(key, 1), array_shape, jnp.float32) * 2.5
    drawn = jnp.clip(drawn, -15.0, 15.0)
    return drawn.astype(jnp.bfloat16)


def draw_key_value_cache(key, part):
    array_shape = (N_SEGMENT, CACHE_SLOTS, 2, VALUE_HEADS * HEAD_SIZE)
    drawn = jnp.clip(jax.random.normal(jax.random.fold_in(key, 5), array_shape, jnp.float32), -6.0, 6.0)
    factor = jnp.where(jnp.arange(2) == 0, 1.0, 2.0)[None, None, :, None]
    drawn = drawn * factor
    return drawn.astype(jnp.bfloat16)


def levels(stream_key, extent, shards, least, high):
    level = 1.0
    for axis_at, parts in shards:
        draws = jax.random.uniform(jax.random.fold_in(jax.random.fold_in(stream_key, 6), axis_at), (parts,), jnp.float32, least / len(shards), high / len(shards))
        level = level * jnp.repeat(jnp.exp(draws), extent[axis_at] // parts).reshape((-1,) + (1,) * (len(extent) - 1 - axis_at))
    return level


def bell_draw(rng, dims, width, most, shards=(), kind=jnp.bfloat16):
    result = jax.random.normal(rng, dims, jnp.float32) * width
    if len(shards) > 0:
        result = levels(rng, dims, shards, -0.22, 0.18) * result
    return jnp.clip(result, min=-most, max=most).astype(kind)


def setup_inputs(seed: int = 0, part: int = 0) -> dict:
    key_of = jax.random.split(jax.random.key(seed), 6)
    part_keys = jax.random.split(jax.random.fold_in(key_of[5], part), 6)
    queries = draw_queries(jax.random.fold_in(jax.random.fold_in(key_of[5], part), 71), part)
    span_key_values = bell_draw(part_keys[1], (N_SEGMENT, SPAN_TOKENS, 2, VALUE_HEADS * HEAD_SIZE), 1.0, 6.0, ((0, 2), (1, 4), (3, 2)))
    key_value_cache = draw_key_value_cache(jax.random.fold_in(jax.random.fold_in(key_of[5], part), 71), part)
    chosen = draw_chosen(jax.random.fold_in(jax.random.fold_in(key_of[5], part), 71), part)
    offset = draw_offset(jax.random.fold_in(jax.random.fold_in(key_of[5], part), 71), part)
    return dict(queries=queries, span_key_values=span_key_values, key_value_cache=key_value_cache, chosen=chosen, offset=offset)


ROPE_BASE = 500000.0


def apply_rotary(values, token_positions):
    half_dim = values.shape[-1] // 2
    frequencies = ROPE_BASE ** (-(2.0 * jnp.arange(half_dim, dtype=jnp.float32)) / values.shape[-1])
    angles = token_positions[:, None] * frequencies[None, :]
    cosine = jnp.cos(angles)[:, None, :]
    sine_part = jnp.sin(angles)[:, None, :]
    widened = values.astype(jnp.float32)
    first_half = widened[..., :half_dim]
    second_half = widened[..., half_dim:]
    joined = jnp.concatenate([first_half * cosine - second_half * sine_part, second_half * cosine + first_half * sine_part], axis=-1)
    return joined.astype(jnp.bfloat16)


def reference(queries, span_key_values, key_value_cache, chosen, offset):
    per_value_head = QUERY_HEADS // VALUE_HEADS
    score_scale = HEAD_SIZE ** -0.5
    results = []
    for layer_section in range(N_SEGMENT):
        token_positions = (offset[layer_section] + jnp.arange(SPAN_TOKENS, dtype=jnp.int32)).astype(jnp.float32)
        rot_query = apply_rotary(queries[layer_section].reshape(SPAN_TOKENS, QUERY_HEADS, HEAD_SIZE), token_positions)
        rotated_key_rows = apply_rotary(span_key_values[layer_section, :, 0].reshape(SPAN_TOKENS, VALUE_HEADS, HEAD_SIZE), token_positions)
        fresh_values = span_key_values[layer_section, :, 1].reshape(SPAN_TOKENS, VALUE_HEADS, HEAD_SIZE)
        stored_entries = key_value_cache[layer_section].reshape(CACHE_BLOCKS, BLOCK_TOKENS, 2, VALUE_HEADS, HEAD_SIZE)
        picked_ids = chosen[layer_section]

        def attend_single_item(index_of_item):
            index_of_item = index_of_item.astype(jnp.int32)
            index_of_block = (index_of_item // VALUE_HEADS).astype(jnp.int32)
            index_of_head = (index_of_item % VALUE_HEADS).astype(jnp.int32)
            zero_index = jnp.zeros((), jnp.int32)
            block_ids = picked_ids[index_of_block, index_of_head]
            fetched = jnp.take(stored_entries, block_ids, axis=0)
            fetched = lax.dynamic_index_in_dim(fetched, index_of_head, axis=3, keepdims=False)
            sel_keys = fetched[:, :, 0].reshape(CHOSEN_BLOCKS * BLOCK_TOKENS, HEAD_SIZE)
            sel_values = fetched[:, :, 1].reshape(CHOSEN_BLOCKS * BLOCK_TOKENS, HEAD_SIZE)
            row_start = (index_of_block * BLOCK_TOKENS).astype(jnp.int32)
            head_start = (index_of_head * per_value_head).astype(jnp.int32)
            own_keys = lax.dynamic_slice(rotated_key_rows, (row_start, index_of_head, zero_index), (BLOCK_TOKENS, 1, HEAD_SIZE)).reshape(BLOCK_TOKENS, HEAD_SIZE)
            own_values = lax.dynamic_slice(fresh_values, (row_start, index_of_head, zero_index), (BLOCK_TOKENS, 1, HEAD_SIZE)).reshape(BLOCK_TOKENS, HEAD_SIZE)
            query_rows = lax.dynamic_slice(rot_query, (row_start, head_start, zero_index), (BLOCK_TOKENS, per_value_head, HEAD_SIZE)).reshape(BLOCK_TOKENS * per_value_head, HEAD_SIZE)
            sel_scores = jnp.dot(query_rows, sel_keys.T, preferred_element_type=jnp.float32) * score_scale
            own_scores = jnp.dot(query_rows, own_keys.T, preferred_element_type=jnp.float32) * score_scale
            query_token = jnp.arange(BLOCK_TOKENS * per_value_head, dtype=jnp.int32) // per_value_head
            key_token = jnp.arange(BLOCK_TOKENS, dtype=jnp.int32)
            causal = key_token[None, :] <= query_token[:, None]
            own_scores = jnp.where(causal, own_scores, -jnp.inf)
            maxima = jnp.maximum(jnp.max(sel_scores, axis=1), jnp.max(own_scores, axis=1))
            sel_weights = jnp.exp(sel_scores - maxima[:, None])
            own_weights = jnp.exp(own_scores - maxima[:, None])
            totals = jnp.sum(sel_weights, axis=1) + jnp.sum(own_weights, axis=1)
            weighted = jnp.dot(sel_weights, sel_values.astype(jnp.float32), precision=lax.Precision.HIGHEST)
            weighted = weighted + jnp.dot(own_weights, own_values.astype(jnp.float32), precision=lax.Precision.HIGHEST)
            context = (weighted / totals[:, None]).astype(jnp.bfloat16)
            return context.reshape(BLOCK_TOKENS, per_value_head, HEAD_SIZE)

        work_items = lax.map(attend_single_item, jnp.arange(QUERY_BLOCKS * VALUE_HEADS, dtype=jnp.int32))
        arranged_rows = work_items.reshape(QUERY_BLOCKS, VALUE_HEADS, BLOCK_TOKENS, per_value_head, HEAD_SIZE).transpose(0, 2, 1, 3, 4)
        results.append(arranged_rows.reshape(SPAN_TOKENS, QUERY_HEADS * HEAD_SIZE))
    stacked = jnp.stack(results)
    return jnp.roll(stacked, 1, axis=0)
```

```python
import functools

import jax
import jax.numpy as jnp
from jax import lax
from jax.experimental import pallas as pl
from jax.experimental.pallas import tpu as pltpu
from jax.sharding import PartitionSpec as P

HEAD_SIZE = 128
BLOCK_TOKENS = 512
CHOSEN_BLOCKS = 8


ROPE_BASE = 500000.0


def swapped(x, axis, stride):
    return lax.ppermute(x, axis, [(i, i ^ 1 << stride) for i in range(lax.axis_size(axis))])


def passed_along(block, axis, distance):
    devices = range(lax.axis_size(axis))
    route = [((i - distance) % len(devices), i) for i in devices]
    return lax.ppermute(block, axis, route)


def apply_rotary(values, token_positions):
    half_dim = values.shape[-1] // 2
    frequencies = ROPE_BASE ** (-(2.0 * jnp.arange(half_dim, dtype=jnp.float32)) / values.shape[-1])
    angles = token_positions[:, None] * frequencies[None, :]
    cosine = jnp.cos(angles)[:, None, :]
    sine_part = jnp.sin(angles)[:, None, :]
    widened = values.astype(jnp.float32)
    first_half = widened[..., :half_dim]
    second_half = widened[..., half_dim:]
    joined = jnp.concatenate(
        [
            first_half * cosine - second_half * sine_part,
            second_half * cosine + first_half * sine_part,
        ],
        axis=-1,
    )
    return joined.astype(jnp.bfloat16)


def combine(earlier, later):
    maxima = jnp.maximum(earlier[0], later[0])
    first_factor = jnp.exp(earlier[0] - maxima)
    second_factor = jnp.exp(later[0] - maxima)
    totals = earlier[1] * first_factor + later[1] * second_factor
    weighted = earlier[2] * first_factor[..., None] + later[2] * second_factor[..., None]
    return (maxima, totals, weighted)


def general(queries, span_key_values, key_value_cache, chosen, offset):
    ctx_size = lax.axis_size("ctx")
    my_index = lax.axis_index("ctx")
    tok_rows = queries.shape[1]
    kv_heads = key_value_cache.shape[3] // HEAD_SIZE
    q_heads = queries.shape[2] // HEAD_SIZE
    per_value_head = q_heads // kv_heads
    members = ctx_size // kv_heads
    blocks_here = key_value_cache.shape[1] // BLOCK_TOKENS
    blocks_total = blocks_here * ctx_size
    q_blocks = chosen.shape[1]
    per_block = BLOCK_TOKENS // tok_rows
    key_rows = BLOCK_TOKENS // members
    own_rows = tok_rows // members
    my_head = my_index // members
    my_rank = my_index % members
    score_scale = HEAD_SIZE ** (-0.5)
    token_start = offset[0] + my_index * tok_rows
    token_positions = (token_start + jnp.arange(tok_rows, dtype=jnp.int32)).astype(jnp.float32)
    rot_query = apply_rotary(queries[0].reshape(tok_rows, q_heads, HEAD_SIZE), token_positions)
    rotated_key_rows = apply_rotary(
        span_key_values[0, :, 0].reshape(tok_rows, kv_heads, HEAD_SIZE), token_positions
    )
    fresh_values = span_key_values[0, :, 1].reshape(tok_rows, kv_heads, HEAD_SIZE)
    query_send = jnp.broadcast_to(
        rot_query.reshape(tok_rows, kv_heads, 1, per_value_head * HEAD_SIZE),
        (tok_rows, kv_heads, members, per_value_head * HEAD_SIZE),
    )
    query_send = query_send.reshape(tok_rows, ctx_size, per_value_head * HEAD_SIZE)
    pair_rows = jnp.concatenate([rotated_key_rows, fresh_values], axis=-1)
    pair_send = (
        pair_rows.reshape(members, own_rows, kv_heads, 2 * HEAD_SIZE)
        .transpose(1, 2, 0, 3)
        .reshape(own_rows, ctx_size, 2 * HEAD_SIZE)
    )
    query_recv, pair_recv = (
        lax.all_to_all(query_send, "ctx", split_axis=1, concat_axis=1, tiled=True),
        lax.all_to_all(pair_send, "ctx", split_axis=1, concat_axis=1, tiled=True),
    )
    picks_here = chosen[0]
    needed = jnp.any(
        picks_here[..., None] == jnp.arange(blocks_total, dtype=jnp.int32), axis=(0, 2)
    )
    needed_here = lax.dynamic_slice_in_dim(needed, my_index * blocks_here, blocks_here, axis=1)
    needed_here = needed_here.T.reshape(blocks_here, 1, kv_heads, 1, 1, 1)
    arranged_rows = (
        key_value_cache[0]
        .reshape(blocks_here, members, key_rows, 2, kv_heads, HEAD_SIZE)
        .transpose(0, 2, 4, 1, 3, 5)
    )
    arranged_rows = jnp.where(needed_here, arranged_rows, jnp.zeros((), jnp.bfloat16))
    tile_send = arranged_rows.reshape(blocks_here * key_rows, ctx_size, 2 * HEAD_SIZE)
    fetched = lax.all_to_all(tile_send, "ctx", split_axis=1, concat_axis=1, tiled=True)
    fetched = fetched.reshape(blocks_here, key_rows, ctx_size, 2 * HEAD_SIZE)
    maxima_parts = []
    totals_parts = []
    weighted_parts = []
    for index_of_block in range(q_blocks):
        block_ids = picks_here[index_of_block][my_head]
        owner_rank = block_ids // blocks_here
        slot_index = block_ids % blocks_here
        picked = fetched[slot_index, :, owner_rank]
        sel_keys = picked[..., :HEAD_SIZE].reshape(CHOSEN_BLOCKS * key_rows, HEAD_SIZE)
        sel_values = picked[..., HEAD_SIZE:].reshape(CHOSEN_BLOCKS * key_rows, HEAD_SIZE)
        first_source = index_of_block * per_block
        own_pairs = pair_recv[:, first_source : first_source + per_block]
        own_keys = own_pairs[..., :HEAD_SIZE].reshape(own_rows * per_block, HEAD_SIZE)
        own_values = own_pairs[..., HEAD_SIZE:].reshape(own_rows * per_block, HEAD_SIZE)
        query_rows = query_recv[:, first_source : first_source + per_block].reshape(
            tok_rows * per_block * per_value_head, HEAD_SIZE
        )
        sources = first_source + jnp.arange(per_block, dtype=jnp.int32)
        query_token = sources[None, :] * tok_rows + jnp.arange(tok_rows, dtype=jnp.int32)[:, None]
        query_token = jnp.broadcast_to(
            query_token[:, :, None], (tok_rows, per_block, per_value_head)
        ).reshape(-1)
        key_token = (
            sources[None, :] * tok_rows
            + my_rank * own_rows
            + jnp.arange(own_rows, dtype=jnp.int32)[:, None]
        )
        key_token = key_token.reshape(-1)
        sel_scores = (
            jnp.dot(query_rows, sel_keys.T, preferred_element_type=jnp.float32) * score_scale
        )
        own_scores = (
            jnp.dot(query_rows, own_keys.T, preferred_element_type=jnp.float32) * score_scale
        )
        causal = key_token[None, :] <= query_token[:, None]
        own_scores = jnp.where(causal, own_scores, -jnp.inf)
        maxima = jnp.maximum(jnp.max(sel_scores, axis=1), jnp.max(own_scores, axis=1))
        sel_weights = jnp.exp(sel_scores - maxima[:, None])
        own_weights = jnp.exp(own_scores - maxima[:, None])
        totals = jnp.sum(sel_weights, axis=1) + jnp.sum(own_weights, axis=1)
        weighted = jnp.dot(
            sel_weights, sel_values.astype(jnp.float32), precision=lax.Precision.HIGHEST
        )
        weighted = weighted + jnp.dot(
            own_weights, own_values.astype(jnp.float32), precision=lax.Precision.HIGHEST
        )
        maxima_parts.append(maxima.reshape(tok_rows, per_block, per_value_head))
        totals_parts.append(totals.reshape(tok_rows, per_block, per_value_head))
        weighted_parts.append(weighted.reshape(tok_rows, per_block, per_value_head, HEAD_SIZE))
    maxima_all = jnp.concatenate(maxima_parts, axis=1)
    totals_all = jnp.concatenate(totals_parts, axis=1)
    weighted_all = jnp.concatenate(weighted_parts, axis=1)
    current = (maxima_all, totals_all, weighted_all)
    bit_count = members.bit_length() - 1
    for bit_index in reversed(range(bit_count)):
        half_rows = current[0].shape[0] // 2
        my_bit = my_index // 2**bit_index % 2
        kept = tuple(
            (
                lax.dynamic_slice_in_dim(part_array, my_bit * half_rows, half_rows, 0)
                for part_array in current
            )
        )
        given = tuple(
            (
                lax.dynamic_slice_in_dim(part_array, (1 - my_bit) * half_rows, half_rows, 0)
                for part_array in current
            )
        )
        partner = swapped((given[0], given[1], given[2]), "ctx", bit_index)
        current = combine(kept, partner)
    finished = (
        (current[2] / current[1][..., None])
        .astype(jnp.bfloat16)
        .reshape(own_rows, ctx_size, per_value_head * HEAD_SIZE)
    )
    returned = lax.all_to_all(finished, "ctx", split_axis=1, concat_axis=1, tiled=True)
    context = (
        returned.reshape(own_rows, kv_heads, members, per_value_head * HEAD_SIZE)
        .transpose(2, 0, 1, 3)
        .reshape(tok_rows, q_heads * HEAD_SIZE)
    )
    handed = passed_along(context, "segment", 1)
    return handed[None]


CHUNKS = 4
LOG2E = 1.4426950408889634
MESH = pl.DeviceIdType.MESH


def attend_kernel(
    n_ctx,
    n_seg,
    chosen_ref,
    q_ref,
    span_ref,
    cache_ref,
    out_ref,
    q_buf,
    span_buf,
    *rest,
):
    kv_bufs = rest[:CHUNKS]
    (k_cat, v_cat, m_buf, acc, tot, done, q_send, q_recv, s_send, s_recv,
     c_send, c_recv, own_sem, o_send, o_recv) = rest[CHUNKS:]
    me = lax.axis_index("ctx")
    seg = lax.axis_index("segment")
    blocks_here = cache_ref.shape[2]
    chunk_rows = cache_ref.shape[4]
    per_head = q_ref.shape[1]
    tokens = q_ref.shape[2]
    after = lax.rem(seg + 1, n_seg)
    before = lax.rem(seg + n_seg - 1, n_seg)
    c2 = LOG2E * HEAD_SIZE ** (-0.5)

    barrier = pltpu.get_barrier_semaphore()
    greeted = 0
    for step in range(1, n_ctx):
        pl.semaphore_signal(
            barrier, inc=1, device_id={"ctx": lax.rem(me + step, n_ctx)}, device_id_type=MESH
        )
        greeted += 1
    for other in (after,) if n_seg == 2 else (after, before):
        for step in range(n_ctx):
            pl.semaphore_signal(
                barrier,
                inc=1,
                device_id={"ctx": lax.rem(me + step, n_ctx), "segment": other},
                device_id_type=MESH,
            )
            greeted += 1
    pl.semaphore_wait(barrier, greeted)

    def to(step):
        return lax.rem(me + step, n_ctx)

    def remote(source, target, send, recv, step):
        return pltpu.make_async_remote_copy(
            src_ref=source,
            dst_ref=target,
            send_sem=send,
            recv_sem=recv,
            device_id={"ctx": to(step)},
            device_id_type=MESH,
        )

    steps = [s for s in (2, 1, 3) if s < n_ctx] + list(range(4, n_ctx))
    mine = pl.ds(me * blocks_here, blocks_here)
    q_copies = [remote(q_ref.at[to(s)], q_buf.at[me], q_send.at[s], q_recv.at[s], s) for s in steps]
    s_copies = [
        remote(span_ref.at[to(s)], span_buf.at[me], s_send.at[s], s_recv.at[s], s) for s in steps
    ]
    c_copies = [
        [
            remote(
                cache_ref.at[c, to(s)], kv_bufs[c].at[mine], c_send.at[c, s], c_recv.at[c, s], s
            )
            for s in steps
        ]
        for c in range(CHUNKS)
    ]
    own_copies = [
        pltpu.make_async_copy(q_ref.at[me], q_buf.at[me], own_sem.at[CHUNKS]),
        pltpu.make_async_copy(span_ref.at[me], span_buf.at[me], own_sem.at[CHUNKS + 1]),
    ] + [
        pltpu.make_async_copy(cache_ref.at[c, me], kv_bufs[c].at[mine], own_sem.at[c])
        for c in range(CHUNKS)
    ]
    for copy in q_copies + s_copies:
        copy.start()
    for copies in c_copies:
        for copy in copies:
            copy.start()
    for copy in own_copies:
        copy.start()

    v_cat[:, HEAD_SIZE:] = jnp.ones((v_cat.shape[0], HEAD_SIZE), v_cat.dtype)

    def fold(b, h, keys, values, causal, first):
        scores = lax.dot_general(
            q_buf[b, h], keys, (((1,), (1,)), ((), ())), preferred_element_type=jnp.float32
        )
        if causal is not None:
            scores = jnp.where(causal, scores, -jnp.inf)
        top = jnp.broadcast_to(jnp.max(scores, axis=1, keepdims=True), (tokens, HEAD_SIZE))
        if not first:
            held = m_buf[b, h]
            top = jnp.maximum(top, held)
        wide = jnp.concatenate([top] * (scores.shape[1] // HEAD_SIZE), axis=1)
        weights = jnp.exp2((scores - wide) * c2).astype(jnp.bfloat16)
        part = jnp.dot(weights, values, preferred_element_type=jnp.float32)
        if first:
            acc[b, h] = part[:, :HEAD_SIZE]
            tot[b, h] = part[:, HEAD_SIZE:]
        else:
            factor = jnp.exp2((held - top) * c2)
            acc[b, h] = acc[b, h] * factor + part[:, :HEAD_SIZE]
            tot[b, h] = tot[b, h] * factor + part[:, HEAD_SIZE:]
        m_buf[b, h] = top

    for copy in q_copies + s_copies:
        copy.wait_recv()
    own_copies[0].wait()
    own_copies[1].wait()

    @pl.loop(0, n_ctx)
    def _(b):
        v_cat[:tokens, :HEAD_SIZE] = span_buf[b, 1]
        rows = lax.broadcasted_iota(jnp.int32, (tokens, tokens), 0)
        columns = lax.broadcasted_iota(jnp.int32, (tokens, tokens), 1)

        @pl.loop(0, per_head)
        def _(h):
            fold(b, h, span_buf[b, 0], v_cat[:tokens], columns <= rows, True)

    def gather(c, b):
        for n in range(CHOSEN_BLOCKS):
            block = chosen_ref[(b * n_ctx + me) * CHOSEN_BLOCKS + n]
            spot = slice(n * chunk_rows, (n + 1) * chunk_rows)
            k_cat[spot, :] = kv_bufs[c][block, 0]
            v_cat[spot, :HEAD_SIZE] = kv_bufs[c][block, 1]

    def out_copy(step):
        return pltpu.make_async_remote_copy(
            src_ref=done.at[step],
            dst_ref=out_ref.at[0, :, pl.ds(pl.multiple_of(me * per_head * HEAD_SIZE, HEAD_SIZE), per_head * HEAD_SIZE)],
            send_sem=o_send.at[step],
            recv_sem=o_recv.at[step],
            device_id={"ctx": to(step), "segment": after},
            device_id_type=MESH,
        )

    for c in range(CHUNKS):
        for copy in c_copies[c]:
            copy.wait_recv()
        own_copies[2 + c].wait()
        if c < CHUNKS - 1:

            @pl.loop(0, n_ctx)
            def _(b):
                gather(c, b)

                @pl.loop(0, per_head)
                def _(h):
                    fold(b, h, k_cat[...], v_cat[...], None, False)

        else:

            @pl.loop(0, n_ctx)
            def _(i):
                step = lax.rem(i + 2, n_ctx)
                b = to(step)
                gather(c, b)
                for h in range(per_head):
                    fold(b, h, k_cat[...], v_cat[...], None, False)
                    done[step, :, h * HEAD_SIZE : (h + 1) * HEAD_SIZE] = (
                        acc[b, h] / tot[b, h]
                    ).astype(done.dtype)
                out_copy(step).start()

    for copies in [q_copies, s_copies] + c_copies:
        for copy in copies:
            copy.wait_send()
    for step in range(n_ctx):
        out_copy(step).wait()


def local(queries, span_key_values, key_value_cache, chosen, offset):
    n_ctx = lax.axis_size("ctx")
    n_seg = lax.axis_size("segment")
    me = lax.axis_index("ctx")
    tokens = queries.shape[1]
    kv_heads = key_value_cache.shape[3] // HEAD_SIZE
    q_heads = queries.shape[2] // HEAD_SIZE
    per_head = q_heads // kv_heads
    if not (n_ctx == kv_heads and tokens == BLOCK_TOKENS and n_seg > 1):
        return general(queries, span_key_values, key_value_cache, chosen, offset)
    blocks_here = key_value_cache.shape[1] // BLOCK_TOKENS
    blocks = blocks_here * n_ctx
    chunk_rows = BLOCK_TOKENS // CHUNKS
    positions = (offset[0] + me * tokens + jnp.arange(tokens, dtype=jnp.int32)).astype(jnp.float32)
    rot_query = apply_rotary(queries[0].reshape(tokens, q_heads, HEAD_SIZE), positions)
    rot_keys = apply_rotary(span_key_values[0, :, 0].reshape(tokens, kv_heads, HEAD_SIZE), positions)
    values = span_key_values[0, :, 1].reshape(tokens, kv_heads, HEAD_SIZE)
    q_send = rot_query.transpose(1, 0, 2).reshape(kv_heads, per_head, tokens, HEAD_SIZE)
    span_send = jnp.stack([rot_keys.transpose(1, 0, 2), values.transpose(1, 0, 2)], axis=1)
    cache_send = (
        key_value_cache[0]
        .reshape(blocks_here, CHUNKS, chunk_rows, 2, kv_heads, HEAD_SIZE)
        .transpose(1, 4, 0, 3, 2, 5)
    )
    bf16, f32 = jnp.bfloat16, jnp.float32
    dma = pltpu.SemaphoreType.DMA
    gathered = CHOSEN_BLOCKS * chunk_rows
    return pl.pallas_call(
        functools.partial(attend_kernel, n_ctx, n_seg),
        out_shape=jax.ShapeDtypeStruct(queries.shape, bf16),
        in_specs=[pl.BlockSpec(memory_space=pltpu.SMEM)] + [pl.BlockSpec(memory_space=pl.ANY)] * 3,
        out_specs=pl.BlockSpec(memory_space=pl.ANY),
        scratch_shapes=[
            pltpu.VMEM((n_ctx, per_head, tokens, HEAD_SIZE), bf16),
            pltpu.VMEM((n_ctx, 2, tokens, HEAD_SIZE), bf16),
        ]
        + [pltpu.VMEM((blocks, 2, chunk_rows, HEAD_SIZE), bf16)] * CHUNKS
        + [
            pltpu.VMEM((gathered, HEAD_SIZE), bf16),
            pltpu.VMEM((max(gathered, tokens), 2 * HEAD_SIZE), bf16),
            pltpu.VMEM((n_ctx, per_head, tokens, HEAD_SIZE), f32),
            pltpu.VMEM((n_ctx, per_head, tokens, HEAD_SIZE), f32),
            pltpu.VMEM((n_ctx, per_head, tokens, HEAD_SIZE), f32),
            pltpu.VMEM((n_ctx, tokens, per_head * HEAD_SIZE), bf16),
            dma((n_ctx,)),
            dma((n_ctx,)),
            dma((n_ctx,)),
            dma((n_ctx,)),
            dma((CHUNKS, n_ctx)),
            dma((CHUNKS, n_ctx)),
            dma((CHUNKS + 2,)),
            dma((n_ctx,)),
            dma((n_ctx,)),
        ],
        compiler_params=pltpu.CompilerParams(
            collective_id=0, has_side_effects=True, vmem_limit_bytes=56 * 2**20
        ),
    )(chosen.reshape(-1), q_send, span_send, cache_send)


def solution(mesh):
    return jax.shard_map(
        local,
        mesh=mesh,
        in_specs=(
            P(("groups", "segment"), "ctx", "head"),
            P(("groups", "segment"), "ctx", None, "head"),
            P(("groups", "segment"), "ctx", None, "head"),
            P(("groups", "segment"), None, "head", None),
            P(("groups", "segment")),
        ),
        out_specs=P(("groups", "segment"), "ctx", "head"),
        check_vma=False,
    )
```

```python
import functools

import jax
import jax.numpy as jnp
from jax import lax
from jax.experimental import pallas as pl
from jax.experimental.pallas import tpu as pltpu
from jax.sharding import PartitionSpec as P

HEAD_SIZE = 128
BLOCK_TOKENS = 512
CHOSEN_BLOCKS = 8


ROPE_BASE = 500000.0


def swapped(x, axis, stride):
    return lax.ppermute(x, axis, [(i, i ^ 1 << stride) for i in range(lax.axis_size(axis))])


def passed_along(block, axis, distance):
    devices = range(lax.axis_size(axis))
    route = [((i - distance) % len(devices), i) for i in devices]
    return lax.ppermute(block, axis, route)


def apply_rotary(values, token_positions):
    half_dim = values.shape[-1] // 2
    frequencies = ROPE_BASE ** (-(2.0 * jnp.arange(half_dim, dtype=jnp.float32)) / values.shape[-1])
    angles = token_positions[:, None] * frequencies[None, :]
    cosine = jnp.cos(angles)[:, None, :]
    sine_part = jnp.sin(angles)[:, None, :]
    widened = values.astype(jnp.float32)
    first_half = widened[..., :half_dim]
    second_half = widened[..., half_dim:]
    joined = jnp.concatenate(
        [
            first_half * cosine - second_half * sine_part,
            second_half * cosine + first_half * sine_part,
        ],
        axis=-1,
    )
    return joined.astype(jnp.bfloat16)


def combine(earlier, later):
    maxima = jnp.maximum(earlier[0], later[0])
    first_factor = jnp.exp(earlier[0] - maxima)
    second_factor = jnp.exp(later[0] - maxima)
    totals = earlier[1] * first_factor + later[1] * second_factor
    weighted = earlier[2] * first_factor[..., None] + later[2] * second_factor[..., None]
    return (maxima, totals, weighted)


def general(queries, span_key_values, key_value_cache, chosen, offset):
    ctx_size = lax.axis_size("ctx")
    my_index = lax.axis_index("ctx")
    tok_rows = queries.shape[1]
    kv_heads = key_value_cache.shape[3] // HEAD_SIZE
    q_heads = queries.shape[2] // HEAD_SIZE
    per_value_head = q_heads // kv_heads
    members = ctx_size // kv_heads
    blocks_here = key_value_cache.shape[1] // BLOCK_TOKENS
    blocks_total = blocks_here * ctx_size
    q_blocks = chosen.shape[1]
    per_block = BLOCK_TOKENS // tok_rows
    key_rows = BLOCK_TOKENS // members
    own_rows = tok_rows // members
    my_head = my_index // members
    my_rank = my_index % members
    score_scale = HEAD_SIZE ** (-0.5)
    token_start = offset[0] + my_index * tok_rows
    token_positions = (token_start + jnp.arange(tok_rows, dtype=jnp.int32)).astype(jnp.float32)
    rot_query = apply_rotary(queries[0].reshape(tok_rows, q_heads, HEAD_SIZE), token_positions)
    rotated_key_rows = apply_rotary(
        span_key_values[0, :, 0].reshape(tok_rows, kv_heads, HEAD_SIZE), token_positions
    )
    fresh_values = span_key_values[0, :, 1].reshape(tok_rows, kv_heads, HEAD_SIZE)
    query_send = jnp.broadcast_to(
        rot_query.reshape(tok_rows, kv_heads, 1, per_value_head * HEAD_SIZE),
        (tok_rows, kv_heads, members, per_value_head * HEAD_SIZE),
    )
    query_send = query_send.reshape(tok_rows, ctx_size, per_value_head * HEAD_SIZE)
    pair_rows = jnp.concatenate([rotated_key_rows, fresh_values], axis=-1)
    pair_send = (
        pair_rows.reshape(members, own_rows, kv_heads, 2 * HEAD_SIZE)
        .transpose(1, 2, 0, 3)
        .reshape(own_rows, ctx_size, 2 * HEAD_SIZE)
    )
    query_recv, pair_recv = (
        lax.all_to_all(query_send, "ctx", split_axis=1, concat_axis=1, tiled=True),
        lax.all_to_all(pair_send, "ctx", split_axis=1, concat_axis=1, tiled=True),
    )
    picks_here = chosen[0]
    needed = jnp.any(
        picks_here[..., None] == jnp.arange(blocks_total, dtype=jnp.int32), axis=(0, 2)
    )
    needed_here = lax.dynamic_slice_in_dim(needed, my_index * blocks_here, blocks_here, axis=1)
    needed_here = needed_here.T.reshape(blocks_here, 1, kv_heads, 1, 1, 1)
    arranged_rows = (
        key_value_cache[0]
        .reshape(blocks_here, members, key_rows, 2, kv_heads, HEAD_SIZE)
        .transpose(0, 2, 4, 1, 3, 5)
    )
    arranged_rows = jnp.where(needed_here, arranged_rows, jnp.zeros((), jnp.bfloat16))
    tile_send = arranged_rows.reshape(blocks_here * key_rows, ctx_size, 2 * HEAD_SIZE)
    fetched = lax.all_to_all(tile_send, "ctx", split_axis=1, concat_axis=1, tiled=True)
    fetched = fetched.reshape(blocks_here, key_rows, ctx_size, 2 * HEAD_SIZE)
    maxima_parts = []
    totals_parts = []
    weighted_parts = []
    for index_of_block in range(q_blocks):
        block_ids = picks_here[index_of_block][my_head]
        owner_rank = block_ids // blocks_here
        slot_index = block_ids % blocks_here
        picked = fetched[slot_index, :, owner_rank]
        sel_keys = picked[..., :HEAD_SIZE].reshape(CHOSEN_BLOCKS * key_rows, HEAD_SIZE)
        sel_values = picked[..., HEAD_SIZE:].reshape(CHOSEN_BLOCKS * key_rows, HEAD_SIZE)
        first_source = index_of_block * per_block
        own_pairs = pair_recv[:, first_source : first_source + per_block]
        own_keys = own_pairs[..., :HEAD_SIZE].reshape(own_rows * per_block, HEAD_SIZE)
        own_values = own_pairs[..., HEAD_SIZE:].reshape(own_rows * per_block, HEAD_SIZE)
        query_rows = query_recv[:, first_source : first_source + per_block].reshape(
            tok_rows * per_block * per_value_head, HEAD_SIZE
        )
        sources = first_source + jnp.arange(per_block, dtype=jnp.int32)
        query_token = sources[None, :] * tok_rows + jnp.arange(tok_rows, dtype=jnp.int32)[:, None]
        query_token = jnp.broadcast_to(
            query_token[:, :, None], (tok_rows, per_block, per_value_head)
        ).reshape(-1)
        key_token = (
            sources[None, :] * tok_rows
            + my_rank * own_rows
            + jnp.arange(own_rows, dtype=jnp.int32)[:, None]
        )
        key_token = key_token.reshape(-1)
        sel_scores = (
            jnp.dot(query_rows, sel_keys.T, preferred_element_type=jnp.float32) * score_scale
        )
        own_scores = (
            jnp.dot(query_rows, own_keys.T, preferred_element_type=jnp.float32) * score_scale
        )
        causal = key_token[None, :] <= query_token[:, None]
        own_scores = jnp.where(causal, own_scores, -jnp.inf)
        maxima = jnp.maximum(jnp.max(sel_scores, axis=1), jnp.max(own_scores, axis=1))
        sel_weights = jnp.exp(sel_scores - maxima[:, None])
        own_weights = jnp.exp(own_scores - maxima[:, None])
        totals = jnp.sum(sel_weights, axis=1) + jnp.sum(own_weights, axis=1)
        weighted = jnp.dot(
            sel_weights, sel_values.astype(jnp.float32), precision=lax.Precision.HIGHEST
        )
        weighted = weighted + jnp.dot(
            own_weights, own_values.astype(jnp.float32), precision=lax.Precision.HIGHEST
        )
        maxima_parts.append(maxima.reshape(tok_rows, per_block, per_value_head))
        totals_parts.append(totals.reshape(tok_rows, per_block, per_value_head))
        weighted_parts.append(weighted.reshape(tok_rows, per_block, per_value_head, HEAD_SIZE))
    maxima_all = jnp.concatenate(maxima_parts, axis=1)
    totals_all = jnp.concatenate(totals_parts, axis=1)
    weighted_all = jnp.concatenate(weighted_parts, axis=1)
    current = (maxima_all, totals_all, weighted_all)
    bit_count = members.bit_length() - 1
    for bit_index in reversed(range(bit_count)):
        half_rows = current[0].shape[0] // 2
        my_bit = my_index // 2**bit_index % 2
        kept = tuple(
            (
                lax.dynamic_slice_in_dim(part_array, my_bit * half_rows, half_rows, 0)
                for part_array in current
            )
        )
        given = tuple(
            (
                lax.dynamic_slice_in_dim(part_array, (1 - my_bit) * half_rows, half_rows, 0)
                for part_array in current
            )
        )
        partner = swapped((given[0], given[1], given[2]), "ctx", bit_index)
        current = combine(kept, partner)
    finished = (
        (current[2] / current[1][..., None])
        .astype(jnp.bfloat16)
        .reshape(own_rows, ctx_size, per_value_head * HEAD_SIZE)
    )
    returned = lax.all_to_all(finished, "ctx", split_axis=1, concat_axis=1, tiled=True)
    context = (
        returned.reshape(own_rows, kv_heads, members, per_value_head * HEAD_SIZE)
        .transpose(2, 0, 1, 3)
        .reshape(tok_rows, q_heads * HEAD_SIZE)
    )
    handed = passed_along(context, "segment", 1)
    return handed[None]


CHUNKS = 4
LOG2E = 1.4426950408889634
MESH = pl.DeviceIdType.MESH


def attend_kernel(
    n_ctx,
    n_seg,
    chosen_ref,
    cos_ref,
    sin_ref,
    q_ref,
    span_ref,
    cache_ref,
    out_ref,
    q_buf,
    span_buf,
    *rest,
):
    kv_bufs = rest[:CHUNKS]
    (k_cat, v_cat, m_buf, acc, tot, done, q_sem, s_send, s_recv,
     c_send, c_recv, own_sem, o_send, o_recv) = rest[CHUNKS:]
    me = lax.axis_index("ctx")
    seg = lax.axis_index("segment")
    blocks_here = cache_ref.shape[2]
    chunk_rows = cache_ref.shape[4]
    per_head = q_ref.shape[2] // HEAD_SIZE
    tokens = q_ref.shape[1]
    after = lax.rem(seg + 1, n_seg)
    before = lax.rem(seg + n_seg - 1, n_seg)
    c2 = LOG2E * HEAD_SIZE ** (-0.5)

    barrier = pltpu.get_barrier_semaphore()
    greeted = 0
    for step in range(1, n_ctx):
        pl.semaphore_signal(
            barrier, inc=1, device_id={"ctx": lax.rem(me + step, n_ctx)}, device_id_type=MESH
        )
        greeted += 1
    for other in (after,) if n_seg == 2 else (after, before):
        for step in range(n_ctx):
            pl.semaphore_signal(
                barrier,
                inc=1,
                device_id={"ctx": lax.rem(me + step, n_ctx), "segment": other},
                device_id_type=MESH,
            )
            greeted += 1
    pl.semaphore_wait(barrier, greeted)

    def to(step):
        return lax.rem(me + step, n_ctx)

    def remote(source, target, send, recv, step):
        return pltpu.make_async_remote_copy(
            src_ref=source,
            dst_ref=target,
            send_sem=send,
            recv_sem=recv,
            device_id={"ctx": to(step)},
            device_id_type=MESH,
        )

    steps = [s for s in (2, 1, 3) if s < n_ctx] + list(range(4, n_ctx))
    mine = pl.ds(me * blocks_here, blocks_here)
    q_copies = [
        pltpu.make_async_copy(
            q_ref.at[b, :, pl.ds(h * HEAD_SIZE, HEAD_SIZE)], q_buf.at[b, h], q_sem.at[b, h]
        )
        for b in range(n_ctx)
        for h in range(per_head)
    ]
    s_copies = [
        remote(span_ref.at[to(s)], span_buf.at[me], s_send.at[s], s_recv.at[s], s) for s in steps
    ]
    c_copies = [
        [
            remote(
                cache_ref.at[c, to(s)], kv_bufs[c].at[mine], c_send.at[c, s], c_recv.at[c, s], s
            )
            for s in steps
        ]
        for c in range(CHUNKS)
    ]
    own_copies = [
        pltpu.make_async_copy(span_ref.at[me], span_buf.at[me], own_sem.at[CHUNKS]),
    ] + [
        pltpu.make_async_copy(cache_ref.at[c, me], kv_bufs[c].at[mine], own_sem.at[c])
        for c in range(CHUNKS)
    ]
    for copy in s_copies:
        copy.start()
    for copies in c_copies:
        for copy in copies:
            copy.start()
    for copy in q_copies + own_copies:
        copy.start()

    v_cat[:, HEAD_SIZE:] = jnp.ones((v_cat.shape[0], HEAD_SIZE), v_cat.dtype)

    def fold(b, h, keys, values, causal, first):
        scores = lax.dot_general(
            q_buf[b, h], keys, (((1,), (1,)), ((), ())), preferred_element_type=jnp.float32
        )
        if causal is not None:
            scores = jnp.where(causal, scores, -jnp.inf)
        top = jnp.broadcast_to(jnp.max(scores, axis=1, keepdims=True), (tokens, HEAD_SIZE))
        if not first:
            held = m_buf[b, h]
            top = jnp.maximum(top, held)
        wide = jnp.concatenate([top] * (scores.shape[1] // HEAD_SIZE), axis=1)
        weights = jnp.exp2((scores - wide) * c2).astype(jnp.bfloat16)
        part = jnp.dot(weights, values, preferred_element_type=jnp.float32)
        if first:
            acc[b, h] = part[:, :HEAD_SIZE]
            tot[b, h] = part[:, HEAD_SIZE:]
        else:
            factor = jnp.exp2((held - top) * c2)
            acc[b, h] = acc[b, h] * factor + part[:, :HEAD_SIZE]
            tot[b, h] = tot[b, h] * factor + part[:, HEAD_SIZE:]
        m_buf[b, h] = top

    def rotated(block, b):
        wide = block.astype(jnp.float32)
        turned = pltpu.roll(wide, HEAD_SIZE // 2, 1)
        return (wide * cos_ref[b] + turned * sin_ref[b]).astype(jnp.bfloat16)

    for copy in q_copies:
        copy.wait()

    @pl.loop(0, n_ctx)
    def _(b):
        @pl.loop(0, per_head)
        def _(h):
            q_buf[b, h] = rotated(q_buf[b, h], b)

    for copy in s_copies:
        copy.wait_recv()
    own_copies[0].wait()

    @pl.loop(0, n_ctx)
    def _(b):
        k_cat[:tokens, :] = rotated(span_buf[b, 0], b)
        v_cat[:tokens, :HEAD_SIZE] = span_buf[b, 1]
        rows = lax.broadcasted_iota(jnp.int32, (tokens, tokens), 0)
        columns = lax.broadcasted_iota(jnp.int32, (tokens, tokens), 1)

        @pl.loop(0, per_head)
        def _(h):
            fold(b, h, k_cat[:tokens], v_cat[:tokens], columns <= rows, True)

    def gather(c, b):
        for n in range(CHOSEN_BLOCKS):
            block = chosen_ref[(b * n_ctx + me) * CHOSEN_BLOCKS + n]
            spot = slice(n * chunk_rows, (n + 1) * chunk_rows)
            k_cat[spot, :] = kv_bufs[c][block, 0]
            v_cat[spot, :HEAD_SIZE] = kv_bufs[c][block, 1]

    def out_copy(step):
        return pltpu.make_async_remote_copy(
            src_ref=done.at[step],
            dst_ref=out_ref.at[0, :, pl.ds(pl.multiple_of(me * per_head * HEAD_SIZE, HEAD_SIZE), per_head * HEAD_SIZE)],
            send_sem=o_send.at[step],
            recv_sem=o_recv.at[step],
            device_id={"ctx": to(step), "segment": after},
            device_id_type=MESH,
        )

    for c in range(CHUNKS):
        for copy in c_copies[c]:
            copy.wait_recv()
        own_copies[1 + c].wait()
        if c < CHUNKS - 1:

            @pl.loop(0, n_ctx)
            def _(b):
                gather(c, b)

                @pl.loop(0, per_head)
                def _(h):
                    fold(b, h, k_cat[...], v_cat[...], None, False)

        else:

            @pl.loop(0, n_ctx)
            def _(i):
                step = lax.rem(i + 2, n_ctx)
                b = to(step)
                gather(c, b)
                for h in range(per_head):
                    fold(b, h, k_cat[...], v_cat[...], None, False)
                    done[step, :, h * HEAD_SIZE : (h + 1) * HEAD_SIZE] = (
                        acc[b, h] / tot[b, h]
                    ).astype(done.dtype)
                out_copy(step).start()

    for copies in [s_copies] + c_copies:
        for copy in copies:
            copy.wait_send()
    for step in range(n_ctx):
        out_copy(step).wait()


def local(queries, span_key_values, key_value_cache, chosen, offset):
    n_ctx = lax.axis_size("ctx")
    n_seg = lax.axis_size("segment")
    tokens = queries.shape[1]
    kv_heads = key_value_cache.shape[3] // HEAD_SIZE
    q_heads = queries.shape[2] // HEAD_SIZE
    per_head = q_heads // kv_heads
    if not (n_ctx == kv_heads and tokens == BLOCK_TOKENS and n_seg > 1):
        return general(queries, span_key_values, key_value_cache, chosen, offset)
    blocks_here = key_value_cache.shape[1] // BLOCK_TOKENS
    blocks = blocks_here * n_ctx
    chunk_rows = BLOCK_TOKENS // CHUNKS
    q_all = lax.all_to_all(
        queries[0].reshape(tokens, n_ctx, per_head * HEAD_SIZE).transpose(1, 0, 2),
        "ctx",
        split_axis=0,
        concat_axis=0,
        tiled=True,
    )
    positions = (offset[0] + jnp.arange(n_ctx * tokens, dtype=jnp.int32)).astype(jnp.float32)
    half = HEAD_SIZE // 2
    frequencies = ROPE_BASE ** (-(2.0 * jnp.arange(half, dtype=jnp.float32)) / HEAD_SIZE)
    angles = positions[:, None] * frequencies[None, :]
    cosine, sine = jnp.cos(angles), jnp.sin(angles)
    cos_table = jnp.concatenate([cosine, cosine], axis=1).reshape(n_ctx, tokens, HEAD_SIZE)
    sin_table = jnp.concatenate([-sine, sine], axis=1).reshape(n_ctx, tokens, HEAD_SIZE)
    span_send = span_key_values[0].reshape(tokens, 2, kv_heads, HEAD_SIZE).transpose(2, 1, 0, 3)
    cache_send = (
        key_value_cache[0]
        .reshape(blocks_here, CHUNKS, chunk_rows, 2, kv_heads, HEAD_SIZE)
        .transpose(1, 4, 0, 3, 2, 5)
    )
    bf16, f32 = jnp.bfloat16, jnp.float32
    dma = pltpu.SemaphoreType.DMA
    gathered = CHOSEN_BLOCKS * chunk_rows
    return pl.pallas_call(
        functools.partial(attend_kernel, n_ctx, n_seg),
        out_shape=jax.ShapeDtypeStruct(queries.shape, bf16),
        in_specs=[pl.BlockSpec(memory_space=pltpu.SMEM)]
        + [pl.BlockSpec(memory_space=pltpu.VMEM)] * 2
        + [pl.BlockSpec(memory_space=pl.ANY)] * 3,
        out_specs=pl.BlockSpec(memory_space=pl.ANY),
        scratch_shapes=[
            pltpu.VMEM((n_ctx, per_head, tokens, HEAD_SIZE), bf16),
            pltpu.VMEM((n_ctx, 2, tokens, HEAD_SIZE), bf16),
        ]
        + [pltpu.VMEM((blocks, 2, chunk_rows, HEAD_SIZE), bf16)] * CHUNKS
        + [
            pltpu.VMEM((gathered, HEAD_SIZE), bf16),
            pltpu.VMEM((max(gathered, tokens), 2 * HEAD_SIZE), bf16),
            pltpu.VMEM((n_ctx, per_head, tokens, HEAD_SIZE), f32),
            pltpu.VMEM((n_ctx, per_head, tokens, HEAD_SIZE), f32),
            pltpu.VMEM((n_ctx, per_head, tokens, HEAD_SIZE), f32),
            pltpu.VMEM((n_ctx, tokens, per_head * HEAD_SIZE), bf16),
            dma((n_ctx, per_head)),
            dma((n_ctx,)),
            dma((n_ctx,)),
            dma((CHUNKS, n_ctx)),
            dma((CHUNKS, n_ctx)),
            dma((CHUNKS + 1,)),
            dma((n_ctx,)),
            dma((n_ctx,)),
        ],
        compiler_params=pltpu.CompilerParams(
            collective_id=0, has_side_effects=True, vmem_limit_bytes=56 * 2**20
        ),
    )(chosen.reshape(-1), cos_table, sin_table, q_all, span_send, cache_send)


def solution(mesh):
    return jax.shard_map(
        local,
        mesh=mesh,
        in_specs=(
            P(("groups", "segment"), "ctx", "head"),
            P(("groups", "segment"), "ctx", None, "head"),
            P(("groups", "segment"), "ctx", None, "head"),
            P(("groups", "segment"), None, "head", None),
            P(("groups", "segment")),
        ),
        out_specs=P(("groups", "segment"), "ctx", "head"),
        check_vma=False,
    )
```

```python
import functools

import jax
import jax.numpy as jnp
from jax import lax
from jax.experimental import pallas as pl
from jax.experimental.pallas import tpu as pltpu
from jax.sharding import PartitionSpec as P

HEAD_SIZE = 128
BLOCK_TOKENS = 512
CHOSEN_BLOCKS = 8


ROPE_BASE = 500000.0


def swapped(x, axis, stride):
    return lax.ppermute(x, axis, [(i, i ^ 1 << stride) for i in range(lax.axis_size(axis))])


def passed_along(block, axis, distance):
    devices = range(lax.axis_size(axis))
    route = [((i - distance) % len(devices), i) for i in devices]
    return lax.ppermute(block, axis, route)


def apply_rotary(values, token_positions):
    half_dim = values.shape[-1] // 2
    frequencies = ROPE_BASE ** (-(2.0 * jnp.arange(half_dim, dtype=jnp.float32)) / values.shape[-1])
    angles = token_positions[:, None] * frequencies[None, :]
    cosine = jnp.cos(angles)[:, None, :]
    sine_part = jnp.sin(angles)[:, None, :]
    widened = values.astype(jnp.float32)
    first_half = widened[..., :half_dim]
    second_half = widened[..., half_dim:]
    joined = jnp.concatenate(
        [
            first_half * cosine - second_half * sine_part,
            second_half * cosine + first_half * sine_part,
        ],
        axis=-1,
    )
    return joined.astype(jnp.bfloat16)


def combine(earlier, later):
    maxima = jnp.maximum(earlier[0], later[0])
    first_factor = jnp.exp(earlier[0] - maxima)
    second_factor = jnp.exp(later[0] - maxima)
    totals = earlier[1] * first_factor + later[1] * second_factor
    weighted = earlier[2] * first_factor[..., None] + later[2] * second_factor[..., None]
    return (maxima, totals, weighted)


def general(queries, span_key_values, key_value_cache, chosen, offset):
    ctx_size = lax.axis_size("ctx")
    my_index = lax.axis_index("ctx")
    tok_rows = queries.shape[1]
    kv_heads = key_value_cache.shape[3] // HEAD_SIZE
    q_heads = queries.shape[2] // HEAD_SIZE
    per_value_head = q_heads // kv_heads
    members = ctx_size // kv_heads
    blocks_here = key_value_cache.shape[1] // BLOCK_TOKENS
    blocks_total = blocks_here * ctx_size
    q_blocks = chosen.shape[1]
    per_block = BLOCK_TOKENS // tok_rows
    key_rows = BLOCK_TOKENS // members
    own_rows = tok_rows // members
    my_head = my_index // members
    my_rank = my_index % members
    score_scale = HEAD_SIZE ** (-0.5)
    token_start = offset[0] + my_index * tok_rows
    token_positions = (token_start + jnp.arange(tok_rows, dtype=jnp.int32)).astype(jnp.float32)
    rot_query = apply_rotary(queries[0].reshape(tok_rows, q_heads, HEAD_SIZE), token_positions)
    rotated_key_rows = apply_rotary(
        span_key_values[0, :, 0].reshape(tok_rows, kv_heads, HEAD_SIZE), token_positions
    )
    fresh_values = span_key_values[0, :, 1].reshape(tok_rows, kv_heads, HEAD_SIZE)
    query_send = jnp.broadcast_to(
        rot_query.reshape(tok_rows, kv_heads, 1, per_value_head * HEAD_SIZE),
        (tok_rows, kv_heads, members, per_value_head * HEAD_SIZE),
    )
    query_send = query_send.reshape(tok_rows, ctx_size, per_value_head * HEAD_SIZE)
    pair_rows = jnp.concatenate([rotated_key_rows, fresh_values], axis=-1)
    pair_send = (
        pair_rows.reshape(members, own_rows, kv_heads, 2 * HEAD_SIZE)
        .transpose(1, 2, 0, 3)
        .reshape(own_rows, ctx_size, 2 * HEAD_SIZE)
    )
    query_recv, pair_recv = (
        lax.all_to_all(query_send, "ctx", split_axis=1, concat_axis=1, tiled=True),
        lax.all_to_all(pair_send, "ctx", split_axis=1, concat_axis=1, tiled=True),
    )
    picks_here = chosen[0]
    needed = jnp.any(
        picks_here[..., None] == jnp.arange(blocks_total, dtype=jnp.int32), axis=(0, 2)
    )
    needed_here = lax.dynamic_slice_in_dim(needed, my_index * blocks_here, blocks_here, axis=1)
    needed_here = needed_here.T.reshape(blocks_here, 1, kv_heads, 1, 1, 1)
    arranged_rows = (
        key_value_cache[0]
        .reshape(blocks_here, members, key_rows, 2, kv_heads, HEAD_SIZE)
        .transpose(0, 2, 4, 1, 3, 5)
    )
    arranged_rows = jnp.where(needed_here, arranged_rows, jnp.zeros((), jnp.bfloat16))
    tile_send = arranged_rows.reshape(blocks_here * key_rows, ctx_size, 2 * HEAD_SIZE)
    fetched = lax.all_to_all(tile_send, "ctx", split_axis=1, concat_axis=1, tiled=True)
    fetched = fetched.reshape(blocks_here, key_rows, ctx_size, 2 * HEAD_SIZE)
    maxima_parts = []
    totals_parts = []
    weighted_parts = []
    for index_of_block in range(q_blocks):
        block_ids = picks_here[index_of_block][my_head]
        owner_rank = block_ids // blocks_here
        slot_index = block_ids % blocks_here
        picked = fetched[slot_index, :, owner_rank]
        sel_keys = picked[..., :HEAD_SIZE].reshape(CHOSEN_BLOCKS * key_rows, HEAD_SIZE)
        sel_values = picked[..., HEAD_SIZE:].reshape(CHOSEN_BLOCKS * key_rows, HEAD_SIZE)
        first_source = index_of_block * per_block
        own_pairs = pair_recv[:, first_source : first_source + per_block]
        own_keys = own_pairs[..., :HEAD_SIZE].reshape(own_rows * per_block, HEAD_SIZE)
        own_values = own_pairs[..., HEAD_SIZE:].reshape(own_rows * per_block, HEAD_SIZE)
        query_rows = query_recv[:, first_source : first_source + per_block].reshape(
            tok_rows * per_block * per_value_head, HEAD_SIZE
        )
        sources = first_source + jnp.arange(per_block, dtype=jnp.int32)
        query_token = sources[None, :] * tok_rows + jnp.arange(tok_rows, dtype=jnp.int32)[:, None]
        query_token = jnp.broadcast_to(
            query_token[:, :, None], (tok_rows, per_block, per_value_head)
        ).reshape(-1)
        key_token = (
            sources[None, :] * tok_rows
            + my_rank * own_rows
            + jnp.arange(own_rows, dtype=jnp.int32)[:, None]
        )
        key_token = key_token.reshape(-1)
        sel_scores = (
            jnp.dot(query_rows, sel_keys.T, preferred_element_type=jnp.float32) * score_scale
        )
        own_scores = (
            jnp.dot(query_rows, own_keys.T, preferred_element_type=jnp.float32) * score_scale
        )
        causal = key_token[None, :] <= query_token[:, None]
        own_scores = jnp.where(causal, own_scores, -jnp.inf)
        maxima = jnp.maximum(jnp.max(sel_scores, axis=1), jnp.max(own_scores, axis=1))
        sel_weights = jnp.exp(sel_scores - maxima[:, None])
        own_weights = jnp.exp(own_scores - maxima[:, None])
        totals = jnp.sum(sel_weights, axis=1) + jnp.sum(own_weights, axis=1)
        weighted = jnp.dot(
            sel_weights, sel_values.astype(jnp.float32), precision=lax.Precision.HIGHEST
        )
        weighted = weighted + jnp.dot(
            own_weights, own_values.astype(jnp.float32), precision=lax.Precision.HIGHEST
        )
        maxima_parts.append(maxima.reshape(tok_rows, per_block, per_value_head))
        totals_parts.append(totals.reshape(tok_rows, per_block, per_value_head))
        weighted_parts.append(weighted.reshape(tok_rows, per_block, per_value_head, HEAD_SIZE))
    maxima_all = jnp.concatenate(maxima_parts, axis=1)
    totals_all = jnp.concatenate(totals_parts, axis=1)
    weighted_all = jnp.concatenate(weighted_parts, axis=1)
    current = (maxima_all, totals_all, weighted_all)
    bit_count = members.bit_length() - 1
    for bit_index in reversed(range(bit_count)):
        half_rows = current[0].shape[0] // 2
        my_bit = my_index // 2**bit_index % 2
        kept = tuple(
            (
                lax.dynamic_slice_in_dim(part_array, my_bit * half_rows, half_rows, 0)
                for part_array in current
            )
        )
        given = tuple(
            (
                lax.dynamic_slice_in_dim(part_array, (1 - my_bit) * half_rows, half_rows, 0)
                for part_array in current
            )
        )
        partner = swapped((given[0], given[1], given[2]), "ctx", bit_index)
        current = combine(kept, partner)
    finished = (
        (current[2] / current[1][..., None])
        .astype(jnp.bfloat16)
        .reshape(own_rows, ctx_size, per_value_head * HEAD_SIZE)
    )
    returned = lax.all_to_all(finished, "ctx", split_axis=1, concat_axis=1, tiled=True)
    context = (
        returned.reshape(own_rows, kv_heads, members, per_value_head * HEAD_SIZE)
        .transpose(2, 0, 1, 3)
        .reshape(tok_rows, q_heads * HEAD_SIZE)
    )
    handed = passed_along(context, "segment", 1)
    return handed[None]


CHUNKS = 8
LOG2E = 1.4426950408889634
MESH = pl.DeviceIdType.MESH


def attend_kernel(
    n_ctx,
    n_seg,
    chosen_ref,
    cos_ref,
    sin_ref,
    q_ref,
    span_ref,
    cache_ref,
    out_ref,
    q_buf,
    span_buf,
    *rest,
):
    kv_bufs = rest[:CHUNKS]
    (k_cat, v_cat, m_buf, acc, tot, done, q_sem, s_send, s_recv,
     c_send, c_recv, own_sem, o_send, o_recv) = rest[CHUNKS:]
    me = lax.axis_index("ctx")
    seg = lax.axis_index("segment")
    blocks_here = cache_ref.shape[2]
    chunk_rows = cache_ref.shape[4]
    per_head = q_ref.shape[2] // HEAD_SIZE
    tokens = q_ref.shape[1]
    after = lax.rem(seg + 1, n_seg)
    before = lax.rem(seg + n_seg - 1, n_seg)
    c2 = LOG2E * HEAD_SIZE ** (-0.5)

    barrier = pltpu.get_barrier_semaphore()
    greeted = 0
    for step in range(1, n_ctx):
        pl.semaphore_signal(
            barrier, inc=1, device_id={"ctx": lax.rem(me + step, n_ctx)}, device_id_type=MESH
        )
        greeted += 1
    for other in (after,) if n_seg == 2 else (after, before):
        for step in range(n_ctx):
            pl.semaphore_signal(
                barrier,
                inc=1,
                device_id={"ctx": lax.rem(me + step, n_ctx), "segment": other},
                device_id_type=MESH,
            )
            greeted += 1
    pl.semaphore_wait(barrier, greeted)

    def to(step):
        return lax.rem(me + step, n_ctx)

    def remote(source, target, send, recv, step):
        return pltpu.make_async_remote_copy(
            src_ref=source,
            dst_ref=target,
            send_sem=send,
            recv_sem=recv,
            device_id={"ctx": to(step)},
            device_id_type=MESH,
        )

    steps = [s for s in (2, 1, 3) if s < n_ctx] + list(range(4, n_ctx))
    mine = pl.ds(me * blocks_here, blocks_here)
    q_copies = [
        pltpu.make_async_copy(
            q_ref.at[b, :, pl.ds(h * HEAD_SIZE, HEAD_SIZE)], q_buf.at[b, h], q_sem.at[b, h]
        )
        for b in range(n_ctx)
        for h in range(per_head)
    ]
    s_copies = [
        remote(span_ref.at[to(s)], span_buf.at[me], s_send.at[s], s_recv.at[s], s) for s in steps
    ]
    c_copies = [
        [
            remote(
                cache_ref.at[c, to(s)], kv_bufs[c].at[mine], c_send.at[c, s], c_recv.at[c, s], s
            )
            for s in steps
        ]
        for c in range(CHUNKS)
    ]
    own_copies = [
        pltpu.make_async_copy(span_ref.at[me], span_buf.at[me], own_sem.at[CHUNKS]),
    ] + [
        pltpu.make_async_copy(cache_ref.at[c, me], kv_bufs[c].at[mine], own_sem.at[c])
        for c in range(CHUNKS)
    ]
    for copy in s_copies:
        copy.start()
    for copies in c_copies:
        for copy in copies:
            copy.start()
    for copy in q_copies + own_copies:
        copy.start()

    v_cat[:, HEAD_SIZE:] = jnp.ones((v_cat.shape[0], HEAD_SIZE), v_cat.dtype)

    def fold(b, h, keys, values, causal, first):
        scores = lax.dot_general(
            q_buf[b, h], keys, (((1,), (1,)), ((), ())), preferred_element_type=jnp.float32
        )
        if causal is not None:
            scores = jnp.where(causal, scores, -jnp.inf)
        top = jnp.broadcast_to(jnp.max(scores, axis=1, keepdims=True), (tokens, HEAD_SIZE))
        if not first:
            held = m_buf[b, h]
            top = jnp.maximum(top, held)
        wide = jnp.concatenate([top] * (scores.shape[1] // HEAD_SIZE), axis=1)
        weights = jnp.exp2((scores - wide) * c2).astype(jnp.bfloat16)
        part = jnp.dot(weights, values, preferred_element_type=jnp.float32)
        if first:
            acc[b, h] = part[:, :HEAD_SIZE]
            tot[b, h] = part[:, HEAD_SIZE:]
        else:
            factor = jnp.exp2((held - top) * c2)
            acc[b, h] = acc[b, h] * factor + part[:, :HEAD_SIZE]
            tot[b, h] = tot[b, h] * factor + part[:, HEAD_SIZE:]
        m_buf[b, h] = top

    def rotated(block, b):
        wide = block.astype(jnp.float32)
        turned = pltpu.roll(wide, HEAD_SIZE // 2, 1)
        return (wide * cos_ref[b] + turned * sin_ref[b]).astype(jnp.bfloat16)

    for copy in q_copies:
        copy.wait()

    @pl.loop(0, n_ctx)
    def _(b):
        @pl.loop(0, per_head)
        def _(h):
            q_buf[b, h] = rotated(q_buf[b, h], b)

    for copy in s_copies:
        copy.wait_recv()
    own_copies[0].wait()

    @pl.loop(0, n_ctx)
    def _(b):
        k_cat[:tokens, :] = rotated(span_buf[b, 0], b)
        v_cat[:tokens, :HEAD_SIZE] = span_buf[b, 1]
        rows = lax.broadcasted_iota(jnp.int32, (tokens, tokens), 0)
        columns = lax.broadcasted_iota(jnp.int32, (tokens, tokens), 1)

        @pl.loop(0, per_head)
        def _(h):
            fold(b, h, k_cat[:tokens], v_cat[:tokens], columns <= rows, True)

    def gather(c, b):
        for n in range(CHOSEN_BLOCKS):
            block = chosen_ref[(b * n_ctx + me) * CHOSEN_BLOCKS + n]
            spot = slice(n * chunk_rows, (n + 1) * chunk_rows)
            k_cat[spot, :] = kv_bufs[c][block, 0]
            v_cat[spot, :HEAD_SIZE] = kv_bufs[c][block, 1]

    def out_copy(step):
        return pltpu.make_async_remote_copy(
            src_ref=done.at[step],
            dst_ref=out_ref.at[0, :, pl.ds(pl.multiple_of(me * per_head * HEAD_SIZE, HEAD_SIZE), per_head * HEAD_SIZE)],
            send_sem=o_send.at[step],
            recv_sem=o_recv.at[step],
            device_id={"ctx": to(step), "segment": after},
            device_id_type=MESH,
        )

    for c in range(CHUNKS):
        for copy in c_copies[c]:
            copy.wait_recv()
        own_copies[1 + c].wait()
        if c < CHUNKS - 1:

            @pl.loop(0, n_ctx)
            def _(b):
                gather(c, b)

                @pl.loop(0, per_head)
                def _(h):
                    fold(b, h, k_cat[...], v_cat[...], None, False)

        else:

            @pl.loop(0, n_ctx)
            def _(i):
                step = lax.rem(i + 2, n_ctx)
                b = to(step)
                gather(c, b)
                for h in range(per_head):
                    fold(b, h, k_cat[...], v_cat[...], None, False)
                    done[step, :, h * HEAD_SIZE : (h + 1) * HEAD_SIZE] = (
                        acc[b, h] / tot[b, h]
                    ).astype(done.dtype)
                out_copy(step).start()

    for copies in [s_copies] + c_copies:
        for copy in copies:
            copy.wait_send()
    for step in range(n_ctx):
        out_copy(step).wait()


def local(queries, span_key_values, key_value_cache, chosen, offset):
    n_ctx = lax.axis_size("ctx")
    n_seg = lax.axis_size("segment")
    tokens = queries.shape[1]
    kv_heads = key_value_cache.shape[3] // HEAD_SIZE
    q_heads = queries.shape[2] // HEAD_SIZE
    per_head = q_heads // kv_heads
    if not (n_ctx == kv_heads and tokens == BLOCK_TOKENS and n_seg > 1):
        return general(queries, span_key_values, key_value_cache, chosen, offset)
    blocks_here = key_value_cache.shape[1] // BLOCK_TOKENS
    blocks = blocks_here * n_ctx
    chunk_rows = BLOCK_TOKENS // CHUNKS
    q_all = lax.all_to_all(
        queries[0].reshape(tokens, n_ctx, per_head * HEAD_SIZE).transpose(1, 0, 2),
        "ctx",
        split_axis=0,
        concat_axis=0,
        tiled=True,
    )
    positions = (offset[0] + jnp.arange(n_ctx * tokens, dtype=jnp.int32)).astype(jnp.float32)
    half = HEAD_SIZE // 2
    frequencies = ROPE_BASE ** (-(2.0 * jnp.arange(half, dtype=jnp.float32)) / HEAD_SIZE)
    angles = positions[:, None] * frequencies[None, :]
    cosine, sine = jnp.cos(angles), jnp.sin(angles)
    cos_table = jnp.concatenate([cosine, cosine], axis=1).reshape(n_ctx, tokens, HEAD_SIZE)
    sin_table = jnp.concatenate([-sine, sine], axis=1).reshape(n_ctx, tokens, HEAD_SIZE)
    span_send = span_key_values[0].reshape(tokens, 2, kv_heads, HEAD_SIZE).transpose(2, 1, 0, 3)
    cache_send = (
        key_value_cache[0]
        .reshape(blocks_here, CHUNKS, chunk_rows, 2, kv_heads, HEAD_SIZE)
        .transpose(1, 4, 0, 3, 2, 5)
    )
    bf16, f32 = jnp.bfloat16, jnp.float32
    dma = pltpu.SemaphoreType.DMA
    gathered = CHOSEN_BLOCKS * chunk_rows
    return pl.pallas_call(
        functools.partial(attend_kernel, n_ctx, n_seg),
        out_shape=jax.ShapeDtypeStruct(queries.shape, bf16),
        in_specs=[pl.BlockSpec(memory_space=pltpu.SMEM)]
        + [pl.BlockSpec(memory_space=pltpu.VMEM)] * 2
        + [pl.BlockSpec(memory_space=pl.ANY)] * 3,
        out_specs=pl.BlockSpec(memory_space=pl.ANY),
        scratch_shapes=[
            pltpu.VMEM((n_ctx, per_head, tokens, HEAD_SIZE), bf16),
            pltpu.VMEM((n_ctx, 2, tokens, HEAD_SIZE), bf16),
        ]
        + [pltpu.VMEM((blocks, 2, chunk_rows, HEAD_SIZE), bf16)] * CHUNKS
        + [
            pltpu.VMEM((gathered, HEAD_SIZE), bf16),
            pltpu.VMEM((max(gathered, tokens), 2 * HEAD_SIZE), bf16),
            pltpu.VMEM((n_ctx, per_head, tokens, HEAD_SIZE), f32),
            pltpu.VMEM((n_ctx, per_head, tokens, HEAD_SIZE), f32),
            pltpu.VMEM((n_ctx, per_head, tokens, HEAD_SIZE), f32),
            pltpu.VMEM((n_ctx, tokens, per_head * HEAD_SIZE), bf16),
            dma((n_ctx, per_head)),
            dma((n_ctx,)),
            dma((n_ctx,)),
            dma((CHUNKS, n_ctx)),
            dma((CHUNKS, n_ctx)),
            dma((CHUNKS + 1,)),
            dma((n_ctx,)),
            dma((n_ctx,)),
        ],
        compiler_params=pltpu.CompilerParams(
            collective_id=0, has_side_effects=True, vmem_limit_bytes=56 * 2**20
        ),
    )(chosen.reshape(-1), cos_table, sin_table, q_all, span_send, cache_send)


def solution(mesh):
    return jax.shard_map(
        local,
        mesh=mesh,
        in_specs=(
            P(("groups", "segment"), "ctx", "head"),
            P(("groups", "segment"), "ctx", None, "head"),
            P(("groups", "segment"), "ctx", None, "head"),
            P(("groups", "segment"), None, "head", None),
            P(("groups", "segment")),
        ),
        out_specs=P(("groups", "segment"), "ctx", "head"),
        check_vma=False,
    )
```
